256 devices in a mesh: gx: 16 (over x_hi, z), gz: 16 (over x_lo, y, core).
Axes of the slice: x: 4 (x_hi: 2, x_lo: 2; x = x_hi * 2 + x_lo), y: 4, z: 8, core: 2. Of those that a mesh axis runs over, the one named last changes fastest.
Arguments:
- direct_modes: bfloat16 [3, 256, 1024, 128], P(None, 'gx', 'gz'), may hold values from -6 to 6
- adjoint_modes: bfloat16 [3, 256, 1024, 128], P(None, 'gx', 'gz'), may hold values from -0.0048828125 to 0.0048828125
- stencil_taps: float32 [36, 256, 1024], P(None, 'gx', 'gz'), may hold values from -0.72 to 0.72
- coupling: float32 [18, 256, 1024], P(None, 'gx', 'gz'), may hold values from -1.2 to 1.2
Outputs:
- evolved: bfloat16 [3, 256, 1024, 128], P(None, 'gx', 'gz')
- reduced: float32 [64, 64], P('gx')
The draws below stay inside these ranges and needn't reach their ends.
All inputs are finite; a program needn't handle non-finite values.
Results may differ from the reference program's by a relative error of at most 0.0031.
Values sent between devices are 32-bit elements; how exact they have to be, the bound alone decides.
A program may use at most 64 MiB of HBM per device.

```python
import jax
import jax.numpy as jnp
from jax import lax

PLANES = 2
MODES = 64
STEPS = 4
NX = 256
NZ = 1024


def steps_of(own_key, dims, cuts, low, high):
    factor_of, own = 1.0, jax.random.fold_in(own_key, 6)
    for axis_at, shards_of in cuts:
        draws = jnp.exp(jax.random.uniform(jax.random.fold_in(own, axis_at), (shards_of,), jnp.float32, low / len(cuts), high / len(cuts)))
        factor_of = factor_of * jnp.repeat(draws, dims[axis_at] // shards_of).reshape([-1 if axis == axis_at else 1 for axis in range(len(dims))])
    return factor_of


def bell_draw(stream_key, shape, deviation, most, cuts=(), held_as=jnp.bfloat16):
    values = deviation * jax.random.normal(stream_key, shape, jnp.float32)
    if cuts:
        values = values * steps_of(stream_key, shape, cuts, -0.22, 0.18)
    return jnp.clip(values, -most, most).astype(held_as)


def setup_inputs(seed: int = 0) -> dict:
    keys = jax.random.split(jax.random.key(seed), 5)
    direct_modes = bell_draw(keys[0], (3, NX, NZ, PLANES * MODES), 1.0, 6.0, ((1, 16), (2, 16)))
    adjoint_modes = bell_draw(keys[1], (3, NX, NZ, PLANES * MODES), (3 * NX * NZ * PLANES) ** -0.5, 0.0048828125, ((1, 16), (2, 16)))
    stencil_taps = bell_draw(keys[2], (PLANES * 18, NX, NZ), 0.12, 0.72, ((1, 16), (2, 16)), jnp.float32)
    coupling = bell_draw(keys[3], (PLANES * 9, NX, NZ), 0.2, 1.2, ((1, 16), (2, 16)), jnp.float32)
    return dict(direct_modes=direct_modes, adjoint_modes=adjoint_modes, stencil_taps=stencil_taps, coupling=coupling)


def advance(padded, tap_block, mix_block):
    width_x = padded.shape[1] - 2
    width_z = padded.shape[2] - 2
    half = padded.shape[3] // 2
    middle = padded[:, 1:1 + width_x, 1:1 + width_z, :]
    outputs = []
    for plane_at in range(2):
        total = jnp.zeros((3, width_x, width_z, half), jnp.float32)
        for side_at in range(2):
            source = plane_at if side_at == 0 else 1 - plane_at
            for tap_at in range(9):
                shift_x = tap_at // 3
                shift_z = tap_at % 3
                shifted = padded[:, shift_x:shift_x + width_x, shift_z:shift_z + width_z, source * half:(source + 1) * half]
                weight = tap_block[plane_at * 18 + side_at * 9 + tap_at]
                total = total + weight[None, :, :, None] * shifted
        own = middle[:, :, :, plane_at * half:(plane_at + 1) * half]
        mixed = []
        for comp_at in range(3):
            term = jnp.zeros((width_x, width_z, half), jnp.float32)
            for other_at in range(3):
                term = term + mix_block[plane_at * 9 + comp_at * 3 + other_at][:, :, None] * own[other_at]
            mixed.append(term)
        outputs.append(own + total + jnp.stack(mixed, axis=0))
    return jnp.concatenate(outputs, axis=3)


def plane_product(adjoint_flat, evolved_flat):
    result = jnp.zeros((adjoint_flat.shape[2], evolved_flat.shape[2]), jnp.float32)
    for plane_at in range(2):
        result = result + lax.dot_general(adjoint_flat[:, plane_at, :], evolved_flat[:, plane_at, :], (((0,), (0,)), ((), ())), preferred_element_type=jnp.float32)
    return result


def reference(direct_modes, adjoint_modes, stencil_taps, coupling):
    split = direct_modes.reshape(3, NX, NZ, 2, MODES)
    adjoint_flat = adjoint_modes.reshape(3 * NX * NZ, 2, MODES)
    block = MODES // 4
    pieces = []
    columns = []
    for block_at in range(4):
        state = split[:, :, :, :, block_at * block:(block_at + 1) * block].reshape(3, NX, NZ, 2 * block).astype(jnp.float32)
        for step in range(STEPS):
            padded = jnp.pad(state, ((0, 0), (1, 1), (1, 1), (0, 0)), mode="wrap")
            state = advance(padded, stencil_taps, coupling)
        evolved_block = state.astype(jnp.bfloat16)
        pieces.append(evolved_block.reshape(3, NX, NZ, 2, block))
        columns.append(plane_product(adjoint_flat, evolved_block.reshape(3 * NX * NZ, 2, block)))
    evolved = jnp.concatenate(pieces, axis=4).reshape(3, NX, NZ, 2 * MODES)
    reduced = jnp.concatenate(columns, axis=1)
    return evolved, reduced
```

```python
import jax
import jax.numpy as jnp
from jax import lax
from jax.sharding import PartitionSpec as P

STEPS = 4


def with_halo(x, sides, width):
    for axis, dim in sides:
        peers, length = (lax.axis_size(axis), x.shape[dim])
        up = [(i, (i + 1) % peers) for i in range(peers)]
        down = [(j, i) for i, j in up]
        last = lax.slice_in_dim(x, length - width, length, axis=dim)
        leading = lax.slice_in_dim(x, 0, width, axis=dim)
        before = lax.ppermute(last, axis, up)
        after = lax.ppermute(leading, axis, down)
        x = jnp.concatenate([before, x, after], axis=dim)
    return x


def lane_weight(lower, first, second):
    return jnp.where(lower, first[:, :, None], second[:, :, None])


def advance(padded, tap_block, mix_block):
    width_x = padded.shape[1] - 2
    width_z = padded.shape[2] - 2
    lanes_all = padded.shape[3]
    half = lanes_all // 2
    lower = lax.broadcasted_iota(jnp.int32, (1, 1, lanes_all), 2) < half
    swapped = jnp.concatenate((padded[:, :, :, half:], padded[:, :, :, :half]), axis=3)
    own = padded[:, 1 : 1 + width_x, 1 : 1 + width_z, :]
    total = jnp.zeros((3, width_x, width_z, lanes_all), jnp.float32)
    for side_at in range(2):
        source = padded if side_at == 0 else swapped
        for tap_at in range(9):
            shift_x = tap_at // 3
            shift_z = tap_at % 3
            shifted = source[:, shift_x : shift_x + width_x, shift_z : shift_z + width_z, :]
            weight = lane_weight(
                lower, tap_block[side_at * 9 + tap_at], tap_block[18 + side_at * 9 + tap_at]
            )
            total = total + weight[None] * shifted
    mixed = []
    for comp_at in range(3):
        term = jnp.zeros((width_x, width_z, lanes_all), jnp.float32)
        for other_at in range(3):
            weight = lane_weight(
                lower, mix_block[comp_at * 3 + other_at], mix_block[9 + comp_at * 3 + other_at]
            )
            term = term + weight * own[other_at]
        mixed.append(term)
    return own + total + jnp.stack(mixed, axis=0)


def plane_product(adjoint_flat, evolved_flat):
    result = jnp.zeros((adjoint_flat.shape[2], evolved_flat.shape[2]), jnp.float32)
    for plane_at in range(2):
        result = result + lax.dot_general(
            adjoint_flat[:, plane_at, :],
            evolved_flat[:, plane_at, :],
            (((0,), (0,)), ((), ())),
            preferred_element_type=jnp.float32,
        )
    return result


def body(direct_modes, adjoint_modes, stencil_taps, coupling):
    state = direct_modes.astype(jnp.float32)
    modes = state.shape[3] // 2
    for step in range(STEPS):
        padded = with_halo(state, (("gx", 1), ("gz", 2)), 1)
        state = advance(padded, stencil_taps, coupling)
    evolved = state.astype(jnp.bfloat16)
    adjoint_flat = adjoint_modes.reshape(-1, 2, modes)
    evolved_flat = evolved.reshape(-1, 2, modes)
    partial_sum = plane_product(adjoint_flat, evolved_flat)
    total = lax.psum(partial_sum, ("gx", "gz"))
    rows = total.shape[0] // lax.axis_size("gx")
    reduced = lax.dynamic_slice_in_dim(total, lax.axis_index("gx") * rows, rows, axis=0)
    return (evolved, reduced)


def solution(mesh):
    placed = (
        P(None, "gx", "gz", None),
        P(None, "gx", "gz", None),
        P(None, "gx", "gz"),
        P(None, "gx", "gz"),
    )
    return jax.shard_map(
        body,
        mesh=mesh,
        in_specs=placed,
        out_specs=(P(None, "gx", "gz", None), P("gx", None)),
        check_vma=False,
    )
```

```python
import jax
import jax.numpy as jnp
from jax import lax
from jax.sharding import PartitionSpec as P

STEPS = 4


def with_halo(x, sides, width):
    for axis, dim in sides:
        peers, length = (lax.axis_size(axis), x.shape[dim])
        up = [(i, (i + 1) % peers) for i in range(peers)]
        down = [(j, i) for i, j in up]
        last = lax.slice_in_dim(x, length - width, length, axis=dim)
        leading = lax.slice_in_dim(x, 0, width, axis=dim)
        before = lax.ppermute(last, axis, up)
        after = lax.ppermute(leading, axis, down)
        x = jnp.concatenate([before, x, after], axis=dim)
    return x


def lane_weight(lower, first, second):
    return jnp.where(lower, first[:, :, None], second[:, :, None])


def advance(padded, tap_block, mix_block):
    width_x = padded.shape[1] - 2
    width_z = padded.shape[2] - 2
    lanes_all = padded.shape[3]
    half = lanes_all // 2
    lower = lax.broadcasted_iota(jnp.int32, (1, 1, lanes_all), 2) < half
    swapped = jnp.concatenate((padded[:, :, :, half:], padded[:, :, :, :half]), axis=3)
    own = padded[:, 1 : 1 + width_x, 1 : 1 + width_z, :]
    total = jnp.zeros((3, width_x, width_z, lanes_all), jnp.float32)
    for side_at in range(2):
        source = padded if side_at == 0 else swapped
        for tap_at in range(9):
            shift_x = tap_at // 3
            shift_z = tap_at % 3
            shifted = source[:, shift_x : shift_x + width_x, shift_z : shift_z + width_z, :]
            weight = lane_weight(
                lower, tap_block[side_at * 9 + tap_at], tap_block[18 + side_at * 9 + tap_at]
            )
            total = total + weight[None] * shifted
    mixed = []
    for comp_at in range(3):
        term = jnp.zeros((width_x, width_z, lanes_all), jnp.float32)
        for other_at in range(3):
            weight = lane_weight(
                lower, mix_block[comp_at * 3 + other_at], mix_block[9 + comp_at * 3 + other_at]
            )
            term = term + weight * own[other_at]
        mixed.append(term)
    return own + total + jnp.stack(mixed, axis=0)


def plane_product(adjoint_flat, evolved_flat):
    result = jnp.zeros((adjoint_flat.shape[2], evolved_flat.shape[2]), jnp.float32)
    for plane_at in range(2):
        result = result + lax.dot_general(
            adjoint_flat[:, plane_at, :],
            evolved_flat[:, plane_at, :],
            (((0,), (0,)), ((), ())),
            preferred_element_type=jnp.float32,
        )
    return result


def body(direct_modes, adjoint_modes, stencil_taps, coupling):
    state = direct_modes.astype(jnp.float32)
    modes = state.shape[3] // 2
    width_x, width_z = state.shape[1], state.shape[2]
    sides = (("gx", 1), ("gz", 2))
    depth = 2
    taps = with_halo(stencil_taps, sides, depth - 1)
    mix = with_halo(coupling, sides, depth - 1)
    for step in range(STEPS):
        rim = depth - 1 - step % depth
        if step % depth == 0:
            padded = with_halo(state, sides, depth)
        at = depth - 1 - rim
        window = (slice(None), slice(at, at + width_x + 2 * rim), slice(at, at + width_z + 2 * rim))
        padded = advance(padded, taps[window], mix[window])
        state = padded
    evolved = state.astype(jnp.bfloat16)
    adjoint_flat = adjoint_modes.reshape(-1, 2, modes)
    evolved_flat = evolved.reshape(-1, 2, modes)
    partial_sum = plane_product(adjoint_flat, evolved_flat)
    total = lax.psum(partial_sum, ("gx", "gz"))
    rows = total.shape[0] // lax.axis_size("gx")
    reduced = lax.dynamic_slice_in_dim(total, lax.axis_index("gx") * rows, rows, axis=0)
    return (evolved, reduced)


def solution(mesh):
    placed = (
        P(None, "gx", "gz", None),
        P(None, "gx", "gz", None),
        P(None, "gx", "gz"),
        P(None, "gx", "gz"),
    )
    return jax.shard_map(
        body,
        mesh=mesh,
        in_specs=placed,
        out_specs=(P(None, "gx", "gz", None), P("gx", None)),
        check_vma=False,
    )
```

```python
import jax
import jax.numpy as jnp
from jax import lax
from jax.experimental import pallas as pl
from jax.experimental.pallas import tpu as pltpu
from jax.sharding import PartitionSpec as P
import functools

MESH = pl.DeviceIdType.MESH

STEPS = 4


def with_halo(x, sides, width):
    for axis, dim in sides:
        peers, length = (lax.axis_size(axis), x.shape[dim])
        up = [(i, (i + 1) % peers) for i in range(peers)]
        down = [(j, i) for i, j in up]
        last = lax.slice_in_dim(x, length - width, length, axis=dim)
        leading = lax.slice_in_dim(x, 0, width, axis=dim)
        before = lax.ppermute(last, axis, up)
        after = lax.ppermute(leading, axis, down)
        x = jnp.concatenate([before, x, after], axis=dim)
    return x


def lane_weight(lower, first, second):
    return jnp.where(lower, first[:, :, None], second[:, :, None])


def advance(padded, tap_block, mix_block):
    width_x = padded.shape[1] - 2
    width_z = padded.shape[2] - 2
    lanes_all = padded.shape[3]
    half = lanes_all // 2
    lower = lax.broadcasted_iota(jnp.int32, (1, 1, lanes_all), 2) < half
    swapped = jnp.concatenate((padded[:, :, :, half:], padded[:, :, :, :half]), axis=3)
    own = padded[:, 1 : 1 + width_x, 1 : 1 + width_z, :]
    total = jnp.zeros((3, width_x, width_z, lanes_all), jnp.float32)
    for side_at in range(2):
        source = padded if side_at == 0 else swapped
        for tap_at in range(9):
            shift_x = tap_at // 3
            shift_z = tap_at % 3
            shifted = source[:, shift_x : shift_x + width_x, shift_z : shift_z + width_z, :]
            weight = lane_weight(
                lower, tap_block[side_at * 9 + tap_at], tap_block[18 + side_at * 9 + tap_at]
            )
            total = total + weight[None] * shifted
    mixed = []
    for comp_at in range(3):
        term = jnp.zeros((width_x, width_z, lanes_all), jnp.float32)
        for other_at in range(3):
            weight = lane_weight(
                lower, mix_block[comp_at * 3 + other_at], mix_block[9 + comp_at * 3 + other_at]
            )
            term = term + weight * own[other_at]
        mixed.append(term)
    return own + total + jnp.stack(mixed, axis=0)


def plane_product(adjoint_flat, evolved_flat):
    result = jnp.zeros((adjoint_flat.shape[2], evolved_flat.shape[2]), jnp.float32)
    for plane_at in range(2):
        result = result + lax.dot_general(
            adjoint_flat[:, plane_at, :],
            evolved_flat[:, plane_at, :],
            (((0,), (0,)), ((), ())),
            preferred_element_type=jnp.float32,
        )
    return result


def gather_phase(src, slots, send_sem, recv_sem, mine, peer_of, count):
    slots[mine] = src[...]
    outgoing = []
    for k in range(1, count):
        target = lax.rem(mine + k, count)
        copy = pltpu.make_async_remote_copy(
            src_ref=src,
            dst_ref=slots.at[mine],
            send_sem=send_sem.at[k],
            recv_sem=recv_sem.at[mine],
            device_id=peer_of(target),
            device_id_type=MESH,
        )
        copy.start()
        outgoing.append(copy)
    for k in range(1, count):
        source = lax.rem(mine + count - k, count)
        incoming = pltpu.make_async_remote_copy(
            src_ref=src,
            dst_ref=slots.at[source],
            send_sem=send_sem.at[k],
            recv_sem=recv_sem.at[source],
            device_id=peer_of(source),
            device_id_type=MESH,
        )
        incoming.wait_recv()
    total = slots[0]
    for j in range(1, count):
        total = total + slots[j]
    return total, outgoing


def allsum_kernel(nx, nz, part_ref, out_ref, mid, slots_z, slots_x, send_z, recv_z, send_x, recv_x):
    a = lax.axis_index("gx")
    g = lax.axis_index("gz")
    barrier = pltpu.get_barrier_semaphore()
    for k in range(1, nz):
        pl.semaphore_signal(barrier, inc=1, device_id=(a, lax.rem(g + k, nz)), device_id_type=MESH)
    for k in range(1, nx):
        pl.semaphore_signal(barrier, inc=1, device_id=(lax.rem(a + k, nx), g), device_id_type=MESH)
    pl.semaphore_wait(barrier, (nz - 1) + (nx - 1))
    spanned, sent_z = gather_phase(part_ref, slots_z, send_z, recv_z, g, lambda t: (a, t), nz)
    mid[...] = spanned
    total, sent_x = gather_phase(mid, slots_x, send_x, recv_x, a, lambda t: (t, g), nx)
    out_ref[...] = total
    for copy in sent_z + sent_x:
        copy.wait_send()


def allsum(part, nx, nz):
    shape = part.shape
    return pl.pallas_call(
        functools.partial(allsum_kernel, nx, nz),
        out_shape=jax.ShapeDtypeStruct(shape, jnp.float32),
        in_specs=[pl.BlockSpec(memory_space=pltpu.VMEM)],
        out_specs=pl.BlockSpec(memory_space=pltpu.VMEM),
        scratch_shapes=[
            pltpu.VMEM(shape, jnp.float32),
            pltpu.VMEM((nz,) + shape, jnp.float32),
            pltpu.VMEM((nx,) + shape, jnp.float32),
            pltpu.SemaphoreType.DMA((nz,)),
            pltpu.SemaphoreType.DMA((nz,)),
            pltpu.SemaphoreType.DMA((nx,)),
            pltpu.SemaphoreType.DMA((nx,)),
        ],
        compiler_params=pltpu.CompilerParams(collective_id=0, has_side_effects=True),
    )(part)


def body(direct_modes, adjoint_modes, stencil_taps, coupling):
    state = direct_modes.astype(jnp.float32)
    modes = state.shape[3] // 2
    for step in range(STEPS):
        padded = with_halo(state, (("gx", 1), ("gz", 2)), 1)
        state = advance(padded, stencil_taps, coupling)
    evolved = state.astype(jnp.bfloat16)
    adjoint_flat = adjoint_modes.reshape(-1, 2, modes)
    evolved_flat = evolved.reshape(-1, 2, modes)
    partial_sum = plane_product(adjoint_flat, evolved_flat)
    nx, nz = lax.axis_size("gx"), lax.axis_size("gz")
    rows = partial_sum.shape[0] // nx
    dense = partial_sum.reshape(nx, rows * partial_sum.shape[1])
    total = allsum(dense, nx, nz)
    reduced = lax.dynamic_slice_in_dim(total, lax.axis_index("gx"), 1, axis=0)
    return (evolved, reduced.reshape(rows, partial_sum.shape[1]))


def solution(mesh):
    placed = (
        P(None, "gx", "gz", None),
        P(None, "gx", "gz", None),
        P(None, "gx", "gz"),
        P(None, "gx", "gz"),
    )
    return jax.shard_map(
        body,
        mesh=mesh,
        in_specs=placed,
        out_specs=(P(None, "gx", "gz", None), P("gx", None)),
        check_vma=False,
    )
```

```python
import jax
import jax.numpy as jnp
from jax import lax
from jax.experimental import pallas as pl
from jax.experimental.pallas import tpu as pltpu
from jax.sharding import PartitionSpec as P
import functools

MESH = pl.DeviceIdType.MESH

STEPS = 4


def with_halo(x, sides, width):
    for axis, dim in sides:
        peers, length = (lax.axis_size(axis), x.shape[dim])
        up = [(i, (i + 1) % peers) for i in range(peers)]
        down = [(j, i) for i, j in up]
        last = lax.slice_in_dim(x, length - width, length, axis=dim)
        leading = lax.slice_in_dim(x, 0, width, axis=dim)
        before = lax.ppermute(last, axis, up)
        after = lax.ppermute(leading, axis, down)
        x = jnp.concatenate([before, x, after], axis=dim)
    return x


def lane_weight(lower, first, second):
    return jnp.where(lower, first[:, :, None], second[:, :, None])


def advance(padded, tap_block, mix_block):
    width_x = padded.shape[1] - 2
    width_z = padded.shape[2] - 2
    lanes_all = padded.shape[3]
    half = lanes_all // 2
    lower = lax.broadcasted_iota(jnp.int32, (1, 1, lanes_all), 2) < half
    swapped = jnp.concatenate((padded[:, :, :, half:], padded[:, :, :, :half]), axis=3)
    own = padded[:, 1 : 1 + width_x, 1 : 1 + width_z, :]
    total = jnp.zeros((3, width_x, width_z, lanes_all), jnp.float32)
    for side_at in range(2):
        source = padded if side_at == 0 else swapped
        for tap_at in range(9):
            shift_x = tap_at // 3
            shift_z = tap_at % 3
            shifted = source[:, shift_x : shift_x + width_x, shift_z : shift_z + width_z, :]
            weight = lane_weight(
                lower, tap_block[side_at * 9 + tap_at], tap_block[18 + side_at * 9 + tap_at]
            )
            total = total + weight[None] * shifted
    mixed = []
    for comp_at in range(3):
        term = jnp.zeros((width_x, width_z, lanes_all), jnp.float32)
        for other_at in range(3):
            weight = lane_weight(
                lower, mix_block[comp_at * 3 + other_at], mix_block[9 + comp_at * 3 + other_at]
            )
            term = term + weight * own[other_at]
        mixed.append(term)
    return own + total + jnp.stack(mixed, axis=0)


def plane_product(adjoint_flat, evolved_flat):
    result = jnp.zeros((adjoint_flat.shape[2], evolved_flat.shape[2]), jnp.float32)
    for plane_at in range(2):
        result = result + lax.dot_general(
            adjoint_flat[:, plane_at, :],
            evolved_flat[:, plane_at, :],
            (((0,), (0,)), ((), ())),
            preferred_element_type=jnp.float32,
        )
    return result


def gather_phase(src, slots, send_sem, recv_sem, mine, peer_of, count):
    slots[mine] = src[...]
    outgoing = []
    for k in range(1, count):
        target = lax.rem(mine + k, count)
        copy = pltpu.make_async_remote_copy(
            src_ref=src,
            dst_ref=slots.at[mine],
            send_sem=send_sem.at[k],
            recv_sem=recv_sem.at[mine],
            device_id=peer_of(target),
            device_id_type=MESH,
        )
        copy.start()
        outgoing.append(copy)
    for k in range(1, count):
        source = lax.rem(mine + count - k, count)
        incoming = pltpu.make_async_remote_copy(
            src_ref=src,
            dst_ref=slots.at[source],
            send_sem=send_sem.at[k],
            recv_sem=recv_sem.at[source],
            device_id=peer_of(source),
            device_id_type=MESH,
        )
        incoming.wait_recv()
    total = slots[0]
    for j in range(1, count):
        total = total + slots[j]
    return total, outgoing


def allsum_kernel(nx, nz, part_ref, out_ref, mid, slots_z, slots_x, send_z, recv_z, send_x, recv_x):
    a = lax.axis_index("gx")
    g = lax.axis_index("gz")
    barrier = pltpu.get_barrier_semaphore()
    for k in range(1, nz):
        pl.semaphore_signal(barrier, inc=1, device_id=(a, lax.rem(g + k, nz)), device_id_type=MESH)
    for k in range(1, nx):
        pl.semaphore_signal(barrier, inc=1, device_id=(lax.rem(a + k, nx), g), device_id_type=MESH)
    pl.semaphore_wait(barrier, (nz - 1) + (nx - 1))
    spanned, sent_z = gather_phase(part_ref, slots_z, send_z, recv_z, g, lambda t: (a, t), nz)
    mid[...] = spanned
    total, sent_x = gather_phase(mid, slots_x, send_x, recv_x, a, lambda t: (t, g), nx)
    out_ref[...] = total
    for copy in sent_z + sent_x:
        copy.wait_send()


def allsum(part, nx, nz):
    shape = part.shape
    return pl.pallas_call(
        functools.partial(allsum_kernel, nx, nz),
        out_shape=jax.ShapeDtypeStruct(shape, jnp.float32),
        in_specs=[pl.BlockSpec(memory_space=pltpu.VMEM)],
        out_specs=pl.BlockSpec(memory_space=pltpu.VMEM),
        scratch_shapes=[
            pltpu.VMEM(shape, jnp.float32),
            pltpu.VMEM((nz,) + shape, jnp.float32),
            pltpu.VMEM((nx,) + shape, jnp.float32),
            pltpu.SemaphoreType.DMA((nz,)),
            pltpu.SemaphoreType.DMA((nz,)),
            pltpu.SemaphoreType.DMA((nx,)),
            pltpu.SemaphoreType.DMA((nx,)),
        ],
        compiler_params=pltpu.CompilerParams(collective_id=0, has_side_effects=True),
    )(part)


def body(direct_modes, adjoint_modes, stencil_taps, coupling):
    state = direct_modes.astype(jnp.float32)
    modes = state.shape[3] // 2
    for step in range(STEPS):
        padded = with_halo(state, (("gx", 1), ("gz", 2)), 1)
        state = advance(padded, stencil_taps, coupling)
    evolved = state.astype(jnp.bfloat16)
    lanes_all = 2 * modes
    square = lax.dot_general(
        adjoint_modes.reshape(-1, lanes_all),
        evolved.reshape(-1, lanes_all),
        (((0,), (0,)), ((), ())),
        preferred_element_type=jnp.float32,
    )
    partial_sum = square[:modes, :modes] + square[modes:, modes:]
    nx, nz = lax.axis_size("gx"), lax.axis_size("gz")
    rows = partial_sum.shape[0] // nx
    dense = partial_sum.reshape(nx, rows * partial_sum.shape[1])
    total = allsum(dense, nx, nz)
    reduced = lax.dynamic_slice_in_dim(total, lax.axis_index("gx"), 1, axis=0)
    return (evolved, reduced.reshape(rows, partial_sum.shape[1]))


def solution(mesh):
    placed = (
        P(None, "gx", "gz", None),
        P(None, "gx", "gz", None),
        P(None, "gx", "gz"),
        P(None, "gx", "gz"),
    )
    return jax.shard_map(
        body,
        mesh=mesh,
        in_specs=placed,
        out_specs=(P(None, "gx", "gz", None), P("gx", None)),
        check_vma=False,
    )
```

```python
import jax
import jax.numpy as jnp
from jax import lax
from jax.experimental import pallas as pl
from jax.experimental.pallas import tpu as pltpu
from jax.sharding import PartitionSpec as P
import functools

MESH = pl.DeviceIdType.MESH

STEPS = 4


def with_halo(x, sides, width):
    for axis, dim in sides:
        peers, length = (lax.axis_size(axis), x.shape[dim])
        up = [(i, (i + 1) % peers) for i in range(peers)]
        down = [(j, i) for i, j in up]
        last = lax.slice_in_dim(x, length - width, length, axis=dim)
        leading = lax.slice_in_dim(x, 0, width, axis=dim)
        before = lax.ppermute(last, axis, up)
        after = lax.ppermute(leading, axis, down)
        x = jnp.concatenate([before, x, after], axis=dim)
    return x


def lane_weight(lower, first, second):
    return jnp.where(lower, first[:, :, None], second[:, :, None])


def advance(padded, tap_block, mix_block):
    width_x = padded.shape[1] - 2
    width_z = padded.shape[2] - 2
    lanes_all = padded.shape[3]
    half = lanes_all // 2
    lower = lax.broadcasted_iota(jnp.int32, (1, 1, lanes_all), 2) < half
    swapped = jnp.concatenate((padded[:, :, :, half:], padded[:, :, :, :half]), axis=3)
    own = padded[:, 1 : 1 + width_x, 1 : 1 + width_z, :]
    total = jnp.zeros((3, width_x, width_z, lanes_all), jnp.float32)
    for side_at in range(2):
        source = padded if side_at == 0 else swapped
        for tap_at in range(9):
            shift_x = tap_at // 3
            shift_z = tap_at % 3
            shifted = source[:, shift_x : shift_x + width_x, shift_z : shift_z + width_z, :]
            weight = lane_weight(
                lower, tap_block[side_at * 9 + tap_at], tap_block[18 + side_at * 9 + tap_at]
            )
            total = total + weight[None] * shifted
    mixed = []
    for comp_at in range(3):
        term = jnp.zeros((width_x, width_z, lanes_all), jnp.float32)
        for other_at in range(3):
            weight = lane_weight(
                lower, mix_block[comp_at * 3 + other_at], mix_block[9 + comp_at * 3 + other_at]
            )
            term = term + weight * own[other_at]
        mixed.append(term)
    return own + total + jnp.stack(mixed, axis=0)


def plane_product(adjoint_flat, evolved_flat):
    result = jnp.zeros((adjoint_flat.shape[2], evolved_flat.shape[2]), jnp.float32)
    for plane_at in range(2):
        result = result + lax.dot_general(
            adjoint_flat[:, plane_at, :],
            evolved_flat[:, plane_at, :],
            (((0,), (0,)), ((), ())),
            preferred_element_type=jnp.float32,
        )
    return result


def gather_phase(src, slots, send_sem, recv_sem, mine, peer_of, count):
    slots[mine] = src[...]
    outgoing = []
    for k in range(1, count):
        target = lax.rem(mine + k, count)
        copy = pltpu.make_async_remote_copy(
            src_ref=src,
            dst_ref=slots.at[mine],
            send_sem=send_sem.at[k],
            recv_sem=recv_sem.at[mine],
            device_id=peer_of(target),
            device_id_type=MESH,
        )
        copy.start()
        outgoing.append(copy)
    for k in range(1, count):
        source = lax.rem(mine + count - k, count)
        incoming = pltpu.make_async_remote_copy(
            src_ref=src,
            dst_ref=slots.at[source],
            send_sem=send_sem.at[k],
            recv_sem=recv_sem.at[source],
            device_id=peer_of(source),
            device_id_type=MESH,
        )
        incoming.wait_recv()
    total = slots[0]
    for j in range(1, count):
        total = total + slots[j]
    return total, outgoing


def allsum_kernel(nx, nz, part_ref, out_ref, mid, slots_z, slots_x, send_z, recv_z, send_x, recv_x):
    a = lax.axis_index("gx")
    g = lax.axis_index("gz")
    barrier = pltpu.get_barrier_semaphore()
    for k in range(1, nz):
        pl.semaphore_signal(barrier, inc=1, device_id=(a, lax.rem(g + k, nz)), device_id_type=MESH)
    for k in range(1, nx):
        pl.semaphore_signal(barrier, inc=1, device_id=(lax.rem(a + k, nx), g), device_id_type=MESH)
    pl.semaphore_wait(barrier, (nz - 1) + (nx - 1))
    spanned, sent_z = gather_phase(part_ref, slots_z, send_z, recv_z, g, lambda t: (a, t), nz)
    mid[...] = spanned
    total, sent_x = gather_phase(mid, slots_x, send_x, recv_x, a, lambda t: (t, g), nx)
    out_ref[...] = total
    for copy in sent_z + sent_x:
        copy.wait_send()


def allsum(part, nx, nz):
    shape = part.shape
    return pl.pallas_call(
        functools.partial(allsum_kernel, nx, nz),
        out_shape=jax.ShapeDtypeStruct(shape, jnp.float32),
        in_specs=[pl.BlockSpec(memory_space=pltpu.VMEM)],
        out_specs=pl.BlockSpec(memory_space=pltpu.VMEM),
        scratch_shapes=[
            pltpu.VMEM(shape, jnp.float32),
            pltpu.VMEM((nz,) + shape, jnp.float32),
            pltpu.VMEM((nx,) + shape, jnp.float32),
            pltpu.SemaphoreType.DMA((nz,)),
            pltpu.SemaphoreType.DMA((nz,)),
            pltpu.SemaphoreType.DMA((nx,)),
            pltpu.SemaphoreType.DMA((nx,)),
        ],
        compiler_params=pltpu.CompilerParams(collective_id=0, has_side_effects=True),
    )(part)


def halo_kernel(nx, nz, rows_ref, cols_ref, corners_ref, rows_in, cols_in, corners_in, send_sem, recv_sem):
    a = lax.axis_index("gx")
    g = lax.axis_index("gz")
    up_x, down_x = lax.rem(a + 1, nx), lax.rem(a + nx - 1, nx)
    up_z, down_z = lax.rem(g + 1, nz), lax.rem(g + nz - 1, nz)
    routes = (
        (rows_ref.at[1], rows_in.at[0], (up_x, g)),
        (rows_ref.at[0], rows_in.at[1], (down_x, g)),
        (cols_ref.at[1], cols_in.at[0], (a, up_z)),
        (cols_ref.at[0], cols_in.at[1], (a, down_z)),
        (corners_ref.at[1, 1], corners_in.at[0, 0], (up_x, up_z)),
        (corners_ref.at[1, 0], corners_in.at[0, 1], (up_x, down_z)),
        (corners_ref.at[0, 1], corners_in.at[1, 0], (down_x, up_z)),
        (corners_ref.at[0, 0], corners_in.at[1, 1], (down_x, down_z)),
    )
    barrier = pltpu.get_barrier_semaphore()
    for _, _, peer in routes:
        pl.semaphore_signal(barrier, inc=1, device_id=peer, device_id_type=MESH)
    pl.semaphore_wait(barrier, len(routes))
    copies = []
    for k, (src, dst, peer) in enumerate(routes):
        copy = pltpu.make_async_remote_copy(
            src_ref=src,
            dst_ref=dst,
            send_sem=send_sem.at[k],
            recv_sem=recv_sem.at[k],
            device_id=peer,
            device_id_type=MESH,
        )
        copy.start()
        copies.append(copy)
    for copy in copies:
        copy.wait_recv()
    for copy in copies:
        copy.wait_send()


def exchange(state, step, nx, nz):
    rows = jnp.stack([state[:, 0], state[:, -1]])
    cols = jnp.stack([state[:, :, 0], state[:, :, -1]])
    corners = jnp.stack(
        [jnp.stack([state[:, 0, 0], state[:, 0, -1]]), jnp.stack([state[:, -1, 0], state[:, -1, -1]])]
    )
    vmem = pl.BlockSpec(memory_space=pltpu.VMEM)
    rows_in, cols_in, corners_in = pl.pallas_call(
        functools.partial(halo_kernel, nx, nz),
        out_shape=(
            jax.ShapeDtypeStruct(rows.shape, rows.dtype),
            jax.ShapeDtypeStruct(cols.shape, cols.dtype),
            jax.ShapeDtypeStruct(corners.shape, corners.dtype),
        ),
        in_specs=[vmem] * 3,
        out_specs=(vmem,) * 3,
        scratch_shapes=[pltpu.SemaphoreType.DMA((8,)), pltpu.SemaphoreType.DMA((8,))],
        compiler_params=pltpu.CompilerParams(collective_id=1 + step, has_side_effects=True),
    )(rows, cols, corners)
    line = lambda left, middle, right: jnp.concatenate(
        [left[:, None, None, :], middle[:, None], right[:, None, None, :]], axis=2
    )
    middle = jnp.concatenate([cols_in[0][:, :, None], state, cols_in[1][:, :, None]], axis=2)
    top = line(corners_in[0, 0], rows_in[0], corners_in[0, 1])
    bottom = line(corners_in[1, 0], rows_in[1], corners_in[1, 1])
    return jnp.concatenate([top, middle, bottom], axis=1)


def body(direct_modes, adjoint_modes, stencil_taps, coupling):
    state = direct_modes.astype(jnp.float32)
    modes = state.shape[3] // 2
    nx, nz = lax.axis_size("gx"), lax.axis_size("gz")
    for step in range(STEPS):
        padded = exchange(state, step, nx, nz)
        state = advance(padded, stencil_taps, coupling)
    evolved = state.astype(jnp.bfloat16)
    lanes_all = 2 * modes
    square = lax.dot_general(
        adjoint_modes.reshape(-1, lanes_all),
        evolved.reshape(-1, lanes_all),
        (((0,), (0,)), ((), ())),
        preferred_element_type=jnp.float32,
    )
    partial_sum = square[:modes, :modes] + square[modes:, modes:]
    rows = partial_sum.shape[0] // nx
    dense = partial_sum.reshape(nx, rows * partial_sum.shape[1])
    total = allsum(dense, nx, nz)
    reduced = lax.dynamic_slice_in_dim(total, lax.axis_index("gx"), 1, axis=0)
    return (evolved, reduced.reshape(rows, partial_sum.shape[1]))


def solution(mesh):
    placed = (
        P(None, "gx", "gz", None),
        P(None, "gx", "gz", None),
        P(None, "gx", "gz"),
        P(None, "gx", "gz"),
    )
    return jax.shard_map(
        body,
        mesh=mesh,
        in_specs=placed,
        out_specs=(P(None, "gx", "gz", None), P("gx", None)),
        check_vma=False,
    )
```

```python
import jax
import jax.numpy as jnp
from jax import lax
from jax.experimental import pallas as pl
from jax.experimental.pallas import tpu as pltpu
from jax.sharding import PartitionSpec as P
import functools

MESH = pl.DeviceIdType.MESH

STEPS = 4


def with_halo(x, sides, width):
    for axis, dim in sides:
        peers, length = (lax.axis_size(axis), x.shape[dim])
        up = [(i, (i + 1) % peers) for i in range(peers)]
        down = [(j, i) for i, j in up]
        last = lax.slice_in_dim(x, length - width, length, axis=dim)
        leading = lax.slice_in_dim(x, 0, width, axis=dim)
        before = lax.ppermute(last, axis, up)
        after = lax.ppermute(leading, axis, down)
        x = jnp.concatenate([before, x, after], axis=dim)
    return x


def lane_weight(lower, first, second):
    return jnp.where(lower, first[:, :, None], second[:, :, None])


def advance(padded, tap_block, mix_block):
    width_x = padded.shape[1] - 2
    width_z = padded.shape[2] - 2
    lanes_all = padded.shape[3]
    half = lanes_all // 2
    lower = lax.broadcasted_iota(jnp.int32, (1, 1, lanes_all), 2) < half
    swapped = jnp.concatenate((padded[:, :, :, half:], padded[:, :, :, :half]), axis=3)
    own = padded[:, 1 : 1 + width_x, 1 : 1 + width_z, :]
    total = jnp.zeros((3, width_x, width_z, lanes_all), jnp.float32)
    for side_at in range(2):
        source = padded if side_at == 0 else swapped
        for tap_at in range(9):
            shift_x = tap_at // 3
            shift_z = tap_at % 3
            shifted = source[:, shift_x : shift_x + width_x, shift_z : shift_z + width_z, :]
            weight = lane_weight(
                lower, tap_block[side_at * 9 + tap_at], tap_block[18 + side_at * 9 + tap_at]
            )
            total = total + weight[None] * shifted
    mixed = []
    for comp_at in range(3):
        term = jnp.zeros((width_x, width_z, lanes_all), jnp.float32)
        for other_at in range(3):
            weight = lane_weight(
                lower, mix_block[comp_at * 3 + other_at], mix_block[9 + comp_at * 3 + other_at]
            )
            term = term + weight * own[other_at]
        mixed.append(term)
    return own + total + jnp.stack(mixed, axis=0)


def plane_product(adjoint_flat, evolved_flat):
    result = jnp.zeros((adjoint_flat.shape[2], evolved_flat.shape[2]), jnp.float32)
    for plane_at in range(2):
        result = result + lax.dot_general(
            adjoint_flat[:, plane_at, :],
            evolved_flat[:, plane_at, :],
            (((0,), (0,)), ((), ())),
            preferred_element_type=jnp.float32,
        )
    return result


def gather_phase(src, slots, send_sem, recv_sem, mine, peer_of, count):
    slots[mine] = src[...]
    outgoing = []
    for k in range(1, count):
        target = lax.rem(mine + k, count)
        copy = pltpu.make_async_remote_copy(
            src_ref=src,
            dst_ref=slots.at[mine],
            send_sem=send_sem.at[k],
            recv_sem=recv_sem.at[mine],
            device_id=peer_of(target),
            device_id_type=MESH,
        )
        copy.start()
        outgoing.append(copy)
    for k in range(1, count):
        source = lax.rem(mine + count - k, count)
        incoming = pltpu.make_async_remote_copy(
            src_ref=src,
            dst_ref=slots.at[source],
            send_sem=send_sem.at[k],
            recv_sem=recv_sem.at[source],
            device_id=peer_of(source),
            device_id_type=MESH,
        )
        incoming.wait_recv()
    total = slots[0]
    for j in range(1, count):
        total = total + slots[j]
    return total, outgoing


def allsum_kernel(nx, nz, part_ref, out_ref, mid, slots_z, slots_x, send_z, recv_z, send_x, recv_x):
    a = lax.axis_index("gx")
    g = lax.axis_index("gz")
    barrier = pltpu.get_barrier_semaphore()
    for k in range(1, nz):
        pl.semaphore_signal(barrier, inc=1, device_id=(a, lax.rem(g + k, nz)), device_id_type=MESH)
    for k in range(1, nx):
        pl.semaphore_signal(barrier, inc=1, device_id=(lax.rem(a + k, nx), g), device_id_type=MESH)
    pl.semaphore_wait(barrier, (nz - 1) + (nx - 1))
    spanned, sent_z = gather_phase(part_ref, slots_z, send_z, recv_z, g, lambda t: (a, t), nz)
    mid[...] = spanned
    total, sent_x = gather_phase(mid, slots_x, send_x, recv_x, a, lambda t: (t, g), nx)
    out_ref[...] = total
    for copy in sent_z + sent_x:
        copy.wait_send()


def allsum(part, nx, nz):
    shape = part.shape
    return pl.pallas_call(
        functools.partial(allsum_kernel, nx, nz),
        out_shape=jax.ShapeDtypeStruct(shape, jnp.float32),
        in_specs=[pl.BlockSpec(memory_space=pltpu.VMEM)],
        out_specs=pl.BlockSpec(memory_space=pltpu.VMEM),
        scratch_shapes=[
            pltpu.VMEM(shape, jnp.float32),
            pltpu.VMEM((nz,) + shape, jnp.float32),
            pltpu.VMEM((nx,) + shape, jnp.float32),
            pltpu.SemaphoreType.DMA((nz,)),
            pltpu.SemaphoreType.DMA((nz,)),
            pltpu.SemaphoreType.DMA((nx,)),
            pltpu.SemaphoreType.DMA((nx,)),
        ],
        compiler_params=pltpu.CompilerParams(collective_id=0, has_side_effects=True),
    )(part)


def body(direct_modes, adjoint_modes, stencil_taps, coupling):
    state = direct_modes.astype(jnp.float32)
    modes = state.shape[3] // 2
    width_x = state.shape[1]
    state = with_halo(state, (("gx", 1),), STEPS)
    fields = with_halo(jnp.concatenate([stencil_taps, coupling], axis=0), (("gx", 1),), STEPS - 1)
    taps, mix = fields[: stencil_taps.shape[0]], fields[stencil_taps.shape[0] :]
    for step in range(STEPS):
        padded = with_halo(state, (("gz", 2),), 1)
        rows = slice(step, step + width_x + 2 * (STEPS - 1 - step))
        state = advance(padded, taps[:, rows], mix[:, rows])
    evolved = state.astype(jnp.bfloat16)
    lanes_all = 2 * modes
    square = lax.dot_general(
        adjoint_modes.reshape(-1, lanes_all),
        evolved.reshape(-1, lanes_all),
        (((0,), (0,)), ((), ())),
        preferred_element_type=jnp.float32,
    )
    partial_sum = square[:modes, :modes] + square[modes:, modes:]
    nx, nz = lax.axis_size("gx"), lax.axis_size("gz")
    rows = partial_sum.shape[0] // nx
    dense = partial_sum.reshape(nx, rows * partial_sum.shape[1])
    total = allsum(dense, nx, nz)
    reduced = lax.dynamic_slice_in_dim(total, lax.axis_index("gx"), 1, axis=0)
    return (evolved, reduced.reshape(rows, partial_sum.shape[1]))


def solution(mesh):
    placed = (
        P(None, "gx", "gz", None),
        P(None, "gx", "gz", None),
        P(None, "gx", "gz"),
        P(None, "gx", "gz"),
    )
    return jax.shard_map(
        body,
        mesh=mesh,
        in_specs=placed,
        out_specs=(P(None, "gx", "gz", None), P("gx", None)),
        check_vma=False,
    )
```

```python
import jax
import jax.numpy as jnp
from jax import lax
from jax.experimental import pallas as pl
from jax.experimental.pallas import tpu as pltpu
from jax.sharding import PartitionSpec as P
import functools

MESH = pl.DeviceIdType.MESH

STEPS = 4


def with_halo(x, sides, width):
    for axis, dim in sides:
        peers, length = (lax.axis_size(axis), x.shape[dim])
        up = [(i, (i + 1) % peers) for i in range(peers)]
        down = [(j, i) for i, j in up]
        last = lax.slice_in_dim(x, length - width, length, axis=dim)
        leading = lax.slice_in_dim(x, 0, width, axis=dim)
        before = lax.ppermute(last, axis, up)
        after = lax.ppermute(leading, axis, down)
        x = jnp.concatenate([before, x, after], axis=dim)
    return x


def lane_weight(lower, first, second):
    return jnp.where(lower, first[:, :, None], second[:, :, None])


def advance(padded, tap_block, mix_block):
    width_x = padded.shape[1] - 2
    width_z = padded.shape[2] - 2
    lanes_all = padded.shape[3]
    half = lanes_all // 2
    lower = lax.broadcasted_iota(jnp.int32, (1, 1, lanes_all), 2) < half
    swapped = jnp.concatenate((padded[:, :, :, half:], padded[:, :, :, :half]), axis=3)
    own = padded[:, 1 : 1 + width_x, 1 : 1 + width_z, :]
    total = jnp.zeros((3, width_x, width_z, lanes_all), jnp.float32)
    for side_at in range(2):
        source = padded if side_at == 0 else swapped
        for tap_at in range(9):
            shift_x = tap_at // 3
            shift_z = tap_at % 3
            shifted = source[:, shift_x : shift_x + width_x, shift_z : shift_z + width_z, :]
            weight = lane_weight(
                lower, tap_block[side_at * 9 + tap_at], tap_block[18 + side_at * 9 + tap_at]
            )
            total = total + weight[None] * shifted
    mixed = []
    for comp_at in range(3):
        term = jnp.zeros((width_x, width_z, lanes_all), jnp.float32)
        for other_at in range(3):
            weight = lane_weight(
                lower, mix_block[comp_at * 3 + other_at], mix_block[9 + comp_at * 3 + other_at]
            )
            term = term + weight * own[other_at]
        mixed.append(term)
    return own + total + jnp.stack(mixed, axis=0)


def plane_product(adjoint_flat, evolved_flat):
    result = jnp.zeros((adjoint_flat.shape[2], evolved_flat.shape[2]), jnp.float32)
    for plane_at in range(2):
        result = result + lax.dot_general(
            adjoint_flat[:, plane_at, :],
            evolved_flat[:, plane_at, :],
            (((0,), (0,)), ((), ())),
            preferred_element_type=jnp.float32,
        )
    return result


def gather_phase(src, slots, send_sem, recv_sem, mine, peer_of, count):
    slots[mine] = src[...]
    outgoing = []
    for k in range(1, count):
        target = lax.rem(mine + k, count)
        copy = pltpu.make_async_remote_copy(
            src_ref=src,
            dst_ref=slots.at[mine],
            send_sem=send_sem.at[k],
            recv_sem=recv_sem.at[mine],
            device_id=peer_of(target),
            device_id_type=MESH,
        )
        copy.start()
        outgoing.append(copy)
    for k in range(1, count):
        source = lax.rem(mine + count - k, count)
        incoming = pltpu.make_async_remote_copy(
            src_ref=src,
            dst_ref=slots.at[source],
            send_sem=send_sem.at[k],
            recv_sem=recv_sem.at[source],
            device_id=peer_of(source),
            device_id_type=MESH,
        )
        incoming.wait_recv()
    total = slots[0]
    for j in range(1, count):
        total = total + slots[j]
    return total, outgoing


def allsum_kernel(nx, nz, part_ref, out_ref, mid, slots_z, slots_x, send_z, recv_z, send_x, recv_x):
    a = lax.axis_index("gx")
    g = lax.axis_index("gz")
    barrier = pltpu.get_barrier_semaphore()
    for k in range(1, nz):
        pl.semaphore_signal(barrier, inc=1, device_id=(a, lax.rem(g + k, nz)), device_id_type=MESH)
    for k in range(1, nx):
        pl.semaphore_signal(barrier, inc=1, device_id=(lax.rem(a + k, nx), g), device_id_type=MESH)
    pl.semaphore_wait(barrier, (nz - 1) + (nx - 1))
    spanned, sent_z = gather_phase(part_ref, slots_z, send_z, recv_z, g, lambda t: (a, t), nz)
    mid[...] = spanned
    total, sent_x = gather_phase(mid, slots_x, send_x, recv_x, a, lambda t: (t, g), nx)
    out_ref[...] = total
    for copy in sent_z + sent_x:
        copy.wait_send()


def allsum(part, nx, nz):
    shape = part.shape
    return pl.pallas_call(
        functools.partial(allsum_kernel, nx, nz),
        out_shape=jax.ShapeDtypeStruct(shape, jnp.float32),
        in_specs=[pl.BlockSpec(memory_space=pltpu.VMEM)],
        out_specs=pl.BlockSpec(memory_space=pltpu.VMEM),
        scratch_shapes=[
            pltpu.VMEM(shape, jnp.float32),
            pltpu.VMEM((nz,) + shape, jnp.float32),
            pltpu.VMEM((nx,) + shape, jnp.float32),
            pltpu.SemaphoreType.DMA((nz,)),
            pltpu.SemaphoreType.DMA((nz,)),
            pltpu.SemaphoreType.DMA((nx,)),
            pltpu.SemaphoreType.DMA((nx,)),
        ],
        compiler_params=pltpu.CompilerParams(collective_id=0, has_side_effects=True),
    )(part)


def step_kernel(padded_ref, weights_ref, out_ref):
    row = pl.program_id(0)
    width_z = out_ref.shape[2]
    half = out_ref.shape[3] // 2
    for comp_at in range(3):
        total = None
        for side_at in range(2):
            for tap_at in range(9):
                shift_x = tap_at // 3
                shift_z = tap_at % 3
                shifted = padded_ref[comp_at, row + shift_x, pl.ds(shift_z, width_z), :]
                if side_at == 1:
                    shifted = pltpu.roll(shifted, half, 1)
                term = weights_ref[side_at * 9 + tap_at, 0] * shifted
                total = term if total is None else total + term
        mixed = None
        for other_at in range(3):
            term = weights_ref[18 + comp_at * 3 + other_at, 0] * padded_ref[other_at, row + 1, pl.ds(1, width_z), :]
            mixed = term if mixed is None else mixed + term
        own = padded_ref[comp_at, row + 1, pl.ds(1, width_z), :]
        out_ref[comp_at, 0] = own + total + mixed


def advance_kernel(padded, weights):
    comps, rows, cols, lanes_all = padded.shape
    width_x, width_z = rows - 2, cols - 2
    return pl.pallas_call(
        step_kernel,
        out_shape=jax.ShapeDtypeStruct((comps, width_x, width_z, lanes_all), jnp.float32),
        grid=(width_x,),
        in_specs=[
            pl.BlockSpec((comps, rows, cols, lanes_all), lambda i: (0, 0, 0, 0)),
            pl.BlockSpec((weights.shape[0], 1, width_z, lanes_all), lambda i: (0, i, 0, 0)),
        ],
        out_specs=pl.BlockSpec((comps, 1, width_z, lanes_all), lambda i: (0, i, 0, 0)),
    )(padded, weights)


def lane_weights(tap_block, mix_block, lanes_all):
    lower = lax.broadcasted_iota(jnp.int32, (1, 1, lanes_all), 2) < lanes_all // 2
    taps = [lane_weight(lower, tap_block[k], tap_block[18 + k]) for k in range(18)]
    mixes = [lane_weight(lower, mix_block[k], mix_block[9 + k]) for k in range(9)]
    return jnp.stack(taps + mixes, axis=0)


def body(direct_modes, adjoint_modes, stencil_taps, coupling):
    state = direct_modes.astype(jnp.float32)
    modes = state.shape[3] // 2
    weights = lane_weights(stencil_taps, coupling, state.shape[3])
    for step in range(STEPS):
        padded = with_halo(state, (("gx", 1), ("gz", 2)), 1)
        state = advance_kernel(padded, weights)
    evolved = state.astype(jnp.bfloat16)
    lanes_all = 2 * modes
    square = lax.dot_general(
        adjoint_modes.reshape(-1, lanes_all),
        evolved.reshape(-1, lanes_all),
        (((0,), (0,)), ((), ())),
        preferred_element_type=jnp.float32,
    )
    partial_sum = square[:modes, :modes] + square[modes:, modes:]
    nx, nz = lax.axis_size("gx"), lax.axis_size("gz")
    rows = partial_sum.shape[0] // nx
    dense = partial_sum.reshape(nx, rows * partial_sum.shape[1])
    total = allsum(dense, nx, nz)
    reduced = lax.dynamic_slice_in_dim(total, lax.axis_index("gx"), 1, axis=0)
    return (evolved, reduced.reshape(rows, partial_sum.shape[1]))


def solution(mesh):
    placed = (
        P(None, "gx", "gz", None),
        P(None, "gx", "gz", None),
        P(None, "gx", "gz"),
        P(None, "gx", "gz"),
    )
    return jax.shard_map(
        body,
        mesh=mesh,
        in_specs=placed,
        out_specs=(P(None, "gx", "gz", None), P("gx", None)),
        check_vma=False,
    )
```

```python
import jax
import jax.numpy as jnp
from jax import lax
from jax.experimental import pallas as pl
from jax.experimental.pallas import tpu as pltpu
from jax.sharding import PartitionSpec as P
import functools

MESH = pl.DeviceIdType.MESH

STEPS = 4


def with_halo(x, sides, width):
    for axis, dim in sides:
        peers, length = (lax.axis_size(axis), x.shape[dim])
        up = [(i, (i + 1) % peers) for i in range(peers)]
        down = [(j, i) for i, j in up]
        last = lax.slice_in_dim(x, length - width, length, axis=dim)
        leading = lax.slice_in_dim(x, 0, width, axis=dim)
        before = lax.ppermute(last, axis, up)
        after = lax.ppermute(leading, axis, down)
        x = jnp.concatenate([before, x, after], axis=dim)
    return x


def lane_weight(lower, first, second):
    return jnp.where(lower, first[:, :, None], second[:, :, None])


def advance(padded, tap_block, mix_block):
    width_x = padded.shape[1] - 2
    width_z = padded.shape[2] - 2
    lanes_all = padded.shape[3]
    half = lanes_all // 2
    lower = lax.broadcasted_iota(jnp.int32, (1, 1, lanes_all), 2) < half
    swapped = jnp.concatenate((padded[:, :, :, half:], padded[:, :, :, :half]), axis=3)
    own = padded[:, 1 : 1 + width_x, 1 : 1 + width_z, :]
    total = jnp.zeros((3, width_x, width_z, lanes_all), jnp.float32)
    for side_at in range(2):
        source = padded if side_at == 0 else swapped
        for tap_at in range(9):
            shift_x = tap_at // 3
            shift_z = tap_at % 3
            shifted = source[:, shift_x : shift_x + width_x, shift_z : shift_z + width_z, :]
            weight = lane_weight(
                lower, tap_block[side_at * 9 + tap_at], tap_block[18 + side_at * 9 + tap_at]
            )
            total = total + weight[None] * shifted
    mixed = []
    for comp_at in range(3):
        term = jnp.zeros((width_x, width_z, lanes_all), jnp.float32)
        for other_at in range(3):
            weight = lane_weight(
                lower, mix_block[comp_at * 3 + other_at], mix_block[9 + comp_at * 3 + other_at]
            )
            term = term + weight * own[other_at]
        mixed.append(term)
    return own + total + jnp.stack(mixed, axis=0)


def advance_weighted(padded, weights):
    width_x = padded.shape[1] - 2
    width_z = padded.shape[2] - 2
    lanes_all = padded.shape[3]
    half = lanes_all // 2
    swapped = jnp.concatenate((padded[:, :, :, half:], padded[:, :, :, :half]), axis=3)
    own = padded[:, 1 : 1 + width_x, 1 : 1 + width_z, :]
    total = jnp.zeros((3, width_x, width_z, lanes_all), jnp.float32)
    for side_at in range(2):
        source = padded if side_at == 0 else swapped
        for tap_at in range(9):
            shift_x = tap_at // 3
            shift_z = tap_at % 3
            shifted = source[:, shift_x : shift_x + width_x, shift_z : shift_z + width_z, :]
            total = total + weights[side_at * 9 + tap_at][None] * shifted
    mixed = []
    for comp_at in range(3):
        term = jnp.zeros((width_x, width_z, lanes_all), jnp.float32)
        for other_at in range(3):
            term = term + weights[18 + comp_at * 3 + other_at] * own[other_at]
        mixed.append(term)
    return own + total + jnp.stack(mixed, axis=0)


def lane_weights(tap_block, mix_block, lanes_all):
    lower = lax.broadcasted_iota(jnp.int32, (1, 1, lanes_all), 2) < lanes_all // 2
    taps = [lane_weight(lower, tap_block[k], tap_block[18 + k]) for k in range(18)]
    mixes = [lane_weight(lower, mix_block[k], mix_block[9 + k]) for k in range(9)]
    return jnp.stack(taps + mixes, axis=0)


def split_step(state, weights):
    ring = lax.axis_size("gx")
    up = [(i, (i + 1) % ring) for i in range(ring)]
    down = [(j, i) for i, j in up]
    spread = with_halo(state, (("gz", 2),), 1)
    before = lax.ppermute(spread[:, -1:], "gx", up)
    after = lax.ppermute(spread[:, :1], "gx", down)
    inner = advance_weighted(spread, weights[:, 1:-1])
    top = advance_weighted(jnp.concatenate([before, spread[:, :2]], axis=1), weights[:, :1])
    bottom = advance_weighted(jnp.concatenate([spread[:, -2:], after], axis=1), weights[:, -1:])
    return jnp.concatenate([top, inner, bottom], axis=1)


def plane_product(adjoint_flat, evolved_flat):
    result = jnp.zeros((adjoint_flat.shape[2], evolved_flat.shape[2]), jnp.float32)
    for plane_at in range(2):
        result = result + lax.dot_general(
            adjoint_flat[:, plane_at, :],
            evolved_flat[:, plane_at, :],
            (((0,), (0,)), ((), ())),
            preferred_element_type=jnp.float32,
        )
    return result


def gather_phase(src, slots, send_sem, recv_sem, mine, peer_of, count):
    slots[mine] = src[...]
    outgoing = []
    for k in range(1, count):
        target = lax.rem(mine + k, count)
        copy = pltpu.make_async_remote_copy(
            src_ref=src,
            dst_ref=slots.at[mine],
            send_sem=send_sem.at[k],
            recv_sem=recv_sem.at[mine],
            device_id=peer_of(target),
            device_id_type=MESH,
        )
        copy.start()
        outgoing.append(copy)
    for k in range(1, count):
        source = lax.rem(mine + count - k, count)
        incoming = pltpu.make_async_remote_copy(
            src_ref=src,
            dst_ref=slots.at[source],
            send_sem=send_sem.at[k],
            recv_sem=recv_sem.at[source],
            device_id=peer_of(source),
            device_id_type=MESH,
        )
        incoming.wait_recv()
    total = slots[0]
    for j in range(1, count):
        total = total + slots[j]
    return total, outgoing


def allsum_kernel(nx, nz, part_ref, out_ref, mid, slots_z, slots_x, send_z, recv_z, send_x, recv_x):
    a = lax.axis_index("gx")
    g = lax.axis_index("gz")
    barrier = pltpu.get_barrier_semaphore()
    for k in range(1, nz):
        pl.semaphore_signal(barrier, inc=1, device_id=(a, lax.rem(g + k, nz)), device_id_type=MESH)
    for k in range(1, nx):
        pl.semaphore_signal(barrier, inc=1, device_id=(lax.rem(a + k, nx), g), device_id_type=MESH)
    pl.semaphore_wait(barrier, (nz - 1) + (nx - 1))
    spanned, sent_z = gather_phase(part_ref, slots_z, send_z, recv_z, g, lambda t: (a, t), nz)
    mid[...] = spanned
    total, sent_x = gather_phase(mid, slots_x, send_x, recv_x, a, lambda t: (t, g), nx)
    out_ref[...] = total
    for copy in sent_z + sent_x:
        copy.wait_send()


def allsum(part, nx, nz):
    shape = part.shape
    return pl.pallas_call(
        functools.partial(allsum_kernel, nx, nz),
        out_shape=jax.ShapeDtypeStruct(shape, jnp.float32),
        in_specs=[pl.BlockSpec(memory_space=pltpu.VMEM)],
        out_specs=pl.BlockSpec(memory_space=pltpu.VMEM),
        scratch_shapes=[
            pltpu.VMEM(shape, jnp.float32),
            pltpu.VMEM((nz,) + shape, jnp.float32),
            pltpu.VMEM((nx,) + shape, jnp.float32),
            pltpu.SemaphoreType.DMA((nz,)),
            pltpu.SemaphoreType.DMA((nz,)),
            pltpu.SemaphoreType.DMA((nx,)),
            pltpu.SemaphoreType.DMA((nx,)),
        ],
        compiler_params=pltpu.CompilerParams(collective_id=0, has_side_effects=True),
    )(part)


def body(direct_modes, adjoint_modes, stencil_taps, coupling):
    state = direct_modes.astype(jnp.float32)
    modes = state.shape[3] // 2
    weights = lane_weights(stencil_taps, coupling, state.shape[3])
    for step in range(STEPS):
        state = split_step(state, weights)
    evolved = state.astype(jnp.bfloat16)
    lanes_all = 2 * modes
    square = lax.dot_general(
        adjoint_modes.reshape(-1, lanes_all),
        evolved.reshape(-1, lanes_all),
        (((0,), (0,)), ((), ())),
        preferred_element_type=jnp.float32,
    )
    partial_sum = square[:modes, :modes] + square[modes:, modes:]
    nx, nz = lax.axis_size("gx"), lax.axis_size("gz")
    rows = partial_sum.shape[0] // nx
    dense = partial_sum.reshape(nx, rows * partial_sum.shape[1])
    total = allsum(dense, nx, nz)
    reduced = lax.dynamic_slice_in_dim(total, lax.axis_index("gx"), 1, axis=0)
    return (evolved, reduced.reshape(rows, partial_sum.shape[1]))


def solution(mesh):
    placed = (
        P(None, "gx", "gz", None),
        P(None, "gx", "gz", None),
        P(None, "gx", "gz"),
        P(None, "gx", "gz"),
    )
    return jax.shard_map(
        body,
        mesh=mesh,
        in_specs=placed,
        out_specs=(P(None, "gx", "gz", None), P("gx", None)),
        check_vma=False,
    )
```

```python
import jax
import jax.numpy as jnp
from jax import lax
from jax.experimental import pallas as pl
from jax.experimental.pallas import tpu as pltpu
from jax.sharding import PartitionSpec as P
import functools

MESH = pl.DeviceIdType.MESH

STEPS = 4


def with_halo(x, sides, width):
    for axis, dim in sides:
        peers, length = (lax.axis_size(axis), x.shape[dim])
        up = [(i, (i + 1) % peers) for i in range(peers)]
        down = [(j, i) for i, j in up]
        last = lax.slice_in_dim(x, length - width, length, axis=dim)
        leading = lax.slice_in_dim(x, 0, width, axis=dim)
        before = lax.ppermute(last, axis, up)
        after = lax.ppermute(leading, axis, down)
        x = jnp.concatenate([before, x, after], axis=dim)
    return x


def lane_weight(lower, first, second):
    return jnp.where(lower, first[:, :, None], second[:, :, None])


def advance(padded, tap_block, mix_block):
    width_x = padded.shape[1] - 2
    width_z = padded.shape[2] - 2
    lanes_all = padded.shape[3]
    half = lanes_all // 2
    lower = lax.broadcasted_iota(jnp.int32, (1, 1, lanes_all), 2) < half
    swapped = jnp.concatenate((padded[:, :, :, half:], padded[:, :, :, :half]), axis=3)
    own = padded[:, 1 : 1 + width_x, 1 : 1 + width_z, :]
    total = jnp.zeros((3, width_x, width_z, lanes_all), jnp.float32)
    for side_at in range(2):
        source = padded if side_at == 0 else swapped
        for tap_at in range(9):
            shift_x = tap_at // 3
            shift_z = tap_at % 3
            shifted = source[:, shift_x : shift_x + width_x, shift_z : shift_z + width_z, :]
            weight = lane_weight(
                lower, tap_block[side_at * 9 + tap_at], tap_block[18 + side_at * 9 + tap_at]
            )
            total = total + weight[None] * shifted
    mixed = []
    for comp_at in range(3):
        term = jnp.zeros((width_x, width_z, lanes_all), jnp.float32)
        for other_at in range(3):
            weight = lane_weight(
                lower, mix_block[comp_at * 3 + other_at], mix_block[9 + comp_at * 3 + other_at]
            )
            term = term + weight * own[other_at]
        mixed.append(term)
    return own + total + jnp.stack(mixed, axis=0)


def plane_product(adjoint_flat, evolved_flat):
    result = jnp.zeros((adjoint_flat.shape[2], evolved_flat.shape[2]), jnp.float32)
    for plane_at in range(2):
        result = result + lax.dot_general(
            adjoint_flat[:, plane_at, :],
            evolved_flat[:, plane_at, :],
            (((0,), (0,)), ((), ())),
            preferred_element_type=jnp.float32,
        )
    return result


def gather_phase(src, slots, send_sem, recv_sem, mine, peer_of, count):
    slots[mine] = src[...]
    outgoing = []
    for k in range(1, count):
        target = lax.rem(mine + k, count)
        copy = pltpu.make_async_remote_copy(
            src_ref=src,
            dst_ref=slots.at[mine],
            send_sem=send_sem.at[k],
            recv_sem=recv_sem.at[mine],
            device_id=peer_of(target),
            device_id_type=MESH,
        )
        copy.start()
        outgoing.append(copy)
    for k in range(1, count):
        source = lax.rem(mine + count - k, count)
        incoming = pltpu.make_async_remote_copy(
            src_ref=src,
            dst_ref=slots.at[source],
            send_sem=send_sem.at[k],
            recv_sem=recv_sem.at[source],
            device_id=peer_of(source),
            device_id_type=MESH,
        )
        incoming.wait_recv()
    total = slots[0]
    for j in range(1, count):
        total = total + slots[j]
    return total, outgoing


def allsum_kernel(nx, nz, part_ref, out_ref, mid, slots_z, slots_x, send_z, recv_z, send_x, recv_x):
    a = lax.axis_index("gx")
    g = lax.axis_index("gz")
    barrier = pltpu.get_barrier_semaphore()
    for k in range(1, nz):
        pl.semaphore_signal(barrier, inc=1, device_id=(a, lax.rem(g + k, nz)), device_id_type=MESH)
    for k in range(1, nx):
        pl.semaphore_signal(barrier, inc=1, device_id=(lax.rem(a + k, nx), g), device_id_type=MESH)
    pl.semaphore_wait(barrier, (nz - 1) + (nx - 1))
    spanned, sent_z = gather_phase(part_ref, slots_z, send_z, recv_z, g, lambda t: (a, t), nz)
    for b in range(nx):
        mid[b] = spanned[b : b + 1]
    slots_x[a] = mid[a]
    sent_x = []
    for k in range(1, nx):
        target = lax.rem(a + k, nx)
        copy = pltpu.make_async_remote_copy(
            src_ref=mid.at[target],
            dst_ref=slots_x.at[a],
            send_sem=send_x.at[k],
            recv_sem=recv_x.at[a],
            device_id=(target, g),
            device_id_type=MESH,
        )
        copy.start()
        sent_x.append(copy)
    for k in range(1, nx):
        source = lax.rem(a + nx - k, nx)
        incoming = pltpu.make_async_remote_copy(
            src_ref=mid.at[source],
            dst_ref=slots_x.at[source],
            send_sem=send_x.at[k],
            recv_sem=recv_x.at[source],
            device_id=(source, g),
            device_id_type=MESH,
        )
        incoming.wait_recv()
    total = slots_x[0]
    for j in range(1, nx):
        total = total + slots_x[j]
    out_ref[...] = total
    for copy in sent_z + sent_x:
        copy.wait_send()


def allsum(part, nx, nz):
    shape = part.shape
    row = (1, shape[1])
    return pl.pallas_call(
        functools.partial(allsum_kernel, nx, nz),
        out_shape=jax.ShapeDtypeStruct(row, jnp.float32),
        in_specs=[pl.BlockSpec(memory_space=pltpu.VMEM)],
        out_specs=pl.BlockSpec(memory_space=pltpu.VMEM),
        scratch_shapes=[
            pltpu.VMEM((nx,) + row, jnp.float32),
            pltpu.VMEM((nz,) + shape, jnp.float32),
            pltpu.VMEM((nx,) + row, jnp.float32),
            pltpu.SemaphoreType.DMA((nz,)),
            pltpu.SemaphoreType.DMA((nz,)),
            pltpu.SemaphoreType.DMA((nx,)),
            pltpu.SemaphoreType.DMA((nx,)),
        ],
        compiler_params=pltpu.CompilerParams(collective_id=0, has_side_effects=True),
    )(part)


def body(direct_modes, adjoint_modes, stencil_taps, coupling):
    state = direct_modes.astype(jnp.float32)
    modes = state.shape[3] // 2
    for step in range(STEPS):
        padded = with_halo(state, (("gx", 1), ("gz", 2)), 1)
        state = advance(padded, stencil_taps, coupling)
    evolved = state.astype(jnp.bfloat16)
    lanes_all = 2 * modes
    square = lax.dot_general(
        adjoint_modes.reshape(-1, lanes_all),
        evolved.reshape(-1, lanes_all),
        (((0,), (0,)), ((), ())),
        preferred_element_type=jnp.float32,
    )
    partial_sum = square[:modes, :modes] + square[modes:, modes:]
    nx, nz = lax.axis_size("gx"), lax.axis_size("gz")
    rows = partial_sum.shape[0] // nx
    dense = partial_sum.reshape(nx, rows * partial_sum.shape[1])
    reduced = allsum(dense, nx, nz)
    return (evolved, reduced.reshape(rows, partial_sum.shape[1]))


def solution(mesh):
    placed = (
        P(None, "gx", "gz", None),
        P(None, "gx", "gz", None),
        P(None, "gx", "gz"),
        P(None, "gx", "gz"),
    )
    return jax.shard_map(
        body,
        mesh=mesh,
        in_specs=placed,
        out_specs=(P(None, "gx", "gz", None), P("gx", None)),
        check_vma=False,
    )
```

```python
import jax
import jax.numpy as jnp
from jax import lax
from jax.experimental import pallas as pl
from jax.experimental.pallas import tpu as pltpu
from jax.sharding import PartitionSpec as P
import functools

MESH = pl.DeviceIdType.MESH

STEPS = 4


def with_halo(x, sides, width):
    for axis, dim in sides:
        peers, length = (lax.axis_size(axis), x.shape[dim])
        up = [(i, (i + 1) % peers) for i in range(peers)]
        down = [(j, i) for i, j in up]
        last = lax.slice_in_dim(x, length - width, length, axis=dim)
        leading = lax.slice_in_dim(x, 0, width, axis=dim)
        before = lax.ppermute(last, axis, up)
        after = lax.ppermute(leading, axis, down)
        x = jnp.concatenate([before, x, after], axis=dim)
    return x


def lane_weight(lower, first, second):
    return jnp.where(lower, first[:, :, None], second[:, :, None])


def advance(padded, tap_block, mix_block):
    width_x = padded.shape[1] - 2
    width_z = padded.shape[2] - 2
    lanes_all = padded.shape[3]
    half = lanes_all // 2
    lower = lax.broadcasted_iota(jnp.int32, (1, 1, lanes_all), 2) < half
    swapped = jnp.concatenate((padded[:, :, :, half:], padded[:, :, :, :half]), axis=3)
    own = padded[:, 1 : 1 + width_x, 1 : 1 + width_z, :]
    total = jnp.zeros((3, width_x, width_z, lanes_all), jnp.float32)
    for side_at in range(2):
        source = padded if side_at == 0 else swapped
        for tap_at in range(9):
            shift_x = tap_at // 3
            shift_z = tap_at % 3
            shifted = source[:, shift_x : shift_x + width_x, shift_z : shift_z + width_z, :]
            weight = lane_weight(
                lower, tap_block[side_at * 9 + tap_at], tap_block[18 + side_at * 9 + tap_at]
            )
            total = total + weight[None] * shifted
    mixed = []
    for comp_at in range(3):
        term = jnp.zeros((width_x, width_z, lanes_all), jnp.float32)
        for other_at in range(3):
            weight = lane_weight(
                lower, mix_block[comp_at * 3 + other_at], mix_block[9 + comp_at * 3 + other_at]
            )
            term = term + weight * own[other_at]
        mixed.append(term)
    return own + total + jnp.stack(mixed, axis=0)


def plane_product(adjoint_flat, evolved_flat):
    result = jnp.zeros((adjoint_flat.shape[2], evolved_flat.shape[2]), jnp.float32)
    for plane_at in range(2):
        result = result + lax.dot_general(
            adjoint_flat[:, plane_at, :],
            evolved_flat[:, plane_at, :],
            (((0,), (0,)), ((), ())),
            preferred_element_type=jnp.float32,
        )
    return result


def gather_phase(src, slots, send_sem, recv_sem, mine, peer_of, count):
    slots[mine] = src[...]
    outgoing = []
    for k in range(1, count):
        target = lax.rem(mine + k, count)
        copy = pltpu.make_async_remote_copy(
            src_ref=src,
            dst_ref=slots.at[mine],
            send_sem=send_sem.at[k],
            recv_sem=recv_sem.at[mine],
            device_id=peer_of(target),
            device_id_type=MESH,
        )
        copy.start()
        outgoing.append(copy)
    for k in range(1, count):
        source = lax.rem(mine + count - k, count)
        incoming = pltpu.make_async_remote_copy(
            src_ref=src,
            dst_ref=slots.at[source],
            send_sem=send_sem.at[k],
            recv_sem=recv_sem.at[source],
            device_id=peer_of(source),
            device_id_type=MESH,
        )
        incoming.wait_recv()
    total = slots[0]
    for j in range(1, count):
        total = total + slots[j]
    return total, outgoing


def allsum_kernel(nx, nz, part_ref, out_ref, mid, slots_x, slots_z, send_x, recv_x, send_z, recv_z):
    a = lax.axis_index("gx")
    g = lax.axis_index("gz")
    barrier = pltpu.get_barrier_semaphore()
    for k in range(1, nz):
        pl.semaphore_signal(barrier, inc=1, device_id=(a, lax.rem(g + k, nz)), device_id_type=MESH)
    for k in range(1, nx):
        pl.semaphore_signal(barrier, inc=1, device_id=(lax.rem(a + k, nx), g), device_id_type=MESH)
    pl.semaphore_wait(barrier, (nz - 1) + (nx - 1))
    slots_x[a] = part_ref[a]
    sent_x = []
    for k in range(1, nx):
        target = lax.rem(a + k, nx)
        copy = pltpu.make_async_remote_copy(
            src_ref=part_ref.at[target],
            dst_ref=slots_x.at[a],
            send_sem=send_x.at[k],
            recv_sem=recv_x.at[a],
            device_id=(target, g),
            device_id_type=MESH,
        )
        copy.start()
        sent_x.append(copy)
    for k in range(1, nx):
        source = lax.rem(a + nx - k, nx)
        incoming = pltpu.make_async_remote_copy(
            src_ref=part_ref.at[source],
            dst_ref=slots_x.at[source],
            send_sem=send_x.at[k],
            recv_sem=recv_x.at[source],
            device_id=(source, g),
            device_id_type=MESH,
        )
        incoming.wait_recv()
    spanned = slots_x[0]
    for j in range(1, nx):
        spanned = spanned + slots_x[j]
    mid[...] = spanned
    total, sent_z = gather_phase(mid, slots_z, send_z, recv_z, g, lambda t: (a, t), nz)
    out_ref[...] = total
    for copy in sent_x + sent_z:
        copy.wait_send()


def allsum(part, nx, nz):
    row = part.shape[1:]
    return pl.pallas_call(
        functools.partial(allsum_kernel, nx, nz),
        out_shape=jax.ShapeDtypeStruct(row, jnp.float32),
        in_specs=[pl.BlockSpec(memory_space=pltpu.VMEM)],
        out_specs=pl.BlockSpec(memory_space=pltpu.VMEM),
        scratch_shapes=[
            pltpu.VMEM(row, jnp.float32),
            pltpu.VMEM((nx,) + row, jnp.float32),
            pltpu.VMEM((nz,) + row, jnp.float32),
            pltpu.SemaphoreType.DMA((nx,)),
            pltpu.SemaphoreType.DMA((nx,)),
            pltpu.SemaphoreType.DMA((nz,)),
            pltpu.SemaphoreType.DMA((nz,)),
        ],
        compiler_params=pltpu.CompilerParams(collective_id=0, has_side_effects=True),
    )(part)


def body(direct_modes, adjoint_modes, stencil_taps, coupling):
    state = direct_modes.astype(jnp.float32)
    modes = state.shape[3] // 2
    for step in range(STEPS):
        padded = with_halo(state, (("gx", 1), ("gz", 2)), 1)
        state = advance(padded, stencil_taps, coupling)
    evolved = state.astype(jnp.bfloat16)
    lanes_all = 2 * modes
    square = lax.dot_general(
        adjoint_modes.reshape(-1, lanes_all),
        evolved.reshape(-1, lanes_all),
        (((0,), (0,)), ((), ())),
        preferred_element_type=jnp.float32,
    )
    partial_sum = square[:modes, :modes] + square[modes:, modes:]
    nx, nz = lax.axis_size("gx"), lax.axis_size("gz")
    rows = partial_sum.shape[0] // nx
    dense = partial_sum.reshape(nx, 1, rows * partial_sum.shape[1])
    reduced = allsum(dense, nx, nz)
    return (evolved, reduced.reshape(rows, partial_sum.shape[1]))


def solution(mesh):
    placed = (
        P(None, "gx", "gz", None),
        P(None, "gx", "gz", None),
        P(None, "gx", "gz"),
        P(None, "gx", "gz"),
    )
    return jax.shard_map(
        body,
        mesh=mesh,
        in_specs=placed,
        out_specs=(P(None, "gx", "gz", None), P("gx", None)),
        check_vma=False,
    )
```
